128 devices in a mesh: grp: 8 (over x_lo, z), row: 16 (over x_hi, y, core).
Axes of the slice: x: 4 (x_hi: 2, x_lo: 2; x = x_hi * 2 + x_lo), y: 4, z: 4, core: 2. Of those that a mesh axis runs over, the one named last changes fastest.
Arguments:
- probes: bfloat16 [8, 8192, 2048], P('grp', 'row'), may hold values from -6 to 6
- solves: bfloat16 [8, 8192, 2048], P('grp', 'row'), may hold values from -6 to 6
- row_spectra: float32 [8, 8192], replicated, may hold values from -0.0625 to 0.0625
- col_spectra: float32 [8, 2048], replicated, may hold values from -0.125 to 0.125
Outputs:
- row_traces: float32 [8, 8192], P(None, ('grp', 'row'))
- col_traces: float32 [8, 2048], replicated
The draws below stay inside these ranges and needn't reach their ends.
All inputs are finite; a program needn't handle non-finite values.
Results may differ from the reference program's by a relative error of at most 0.0003.
Values sent between devices are 32-bit elements; how exact they have to be, the bound alone decides.
A program may use at most 128 MiB of HBM per device.

```python
import jax
import jax.numpy as jnp
from jax import lax

L1 = 8192
L2 = 2048
HYPER = 8
PROBES = 8


def block_scale(key, extent, cuts, least, largest):
    factor_of, own = 1.0, jax.random.fold_in(key, 6)
    for position, shards_of in cuts:
        draws = jnp.exp(jax.random.uniform(jax.random.fold_in(own, position), (shards_of,), jnp.float32, least / len(cuts), largest / len(cuts)))
        factor_of = factor_of * jnp.repeat(draws, extent[position] // shards_of).reshape([-1 if axis == position else 1 for axis in range(len(extent))])
    return factor_of


def centred(rng, shape, spread, reach, pieces=(), kind=jnp.bfloat16):
    gain = block_scale(rng, shape, pieces, -0.22, 0.18) if pieces else 1.0
    values = jax.random.normal(rng, shape, jnp.float32) * spread * gain
    return jnp.minimum(jnp.maximum(values, -reach), reach).astype(kind)


def setup_inputs(seed: int = 0) -> dict:
    arg_keys = jax.random.split(jax.random.key(seed), 5)
    return {
        "probes": centred(arg_keys[0], (PROBES, L1, L2), 1.0, 6.0, ((0, 8), (1, 16))),
        "solves": centred(arg_keys[1], (PROBES, L1, L2), 1.0, 6.0, ((0, 8), (1, 16))),
        "row_spectra": centred(arg_keys[2], (HYPER, L1), L1 ** -0.5, 0.0625, (), jnp.float32),
        "col_spectra": centred(arg_keys[3], (HYPER, L2), L2 ** -0.5, 0.125, (), jnp.float32),
    }


def reference(probes, solves, row_spectra, col_spectra):
    def one_probe(total, pair):
        zhat = jnp.fft.fft2(pair[0].astype(jnp.float32))
        uhat = jnp.fft.fft2(pair[1].astype(jnp.float32))
        term = jnp.real(zhat) * jnp.real(uhat) + jnp.imag(zhat) * jnp.imag(uhat)
        return total + term.astype(total.dtype), None

    start_total = jnp.zeros((L1, L2), jnp.float32)
    total, _ = lax.scan(one_probe, start_total, (probes, solves))
    cross = total / (PROBES * L1 * L2)
    row_traces = jnp.einsum("kj,ij->ki", col_spectra, cross, precision=lax.Precision.HIGHEST)
    col_traces = jnp.einsum("ki,ij->kj", row_spectra, cross, precision=lax.Precision.HIGHEST)
    return row_traces, col_traces
```

```python
import functools
import math

import jax
import jax.numpy as jnp
import ml_dtypes
import numpy as np
from jax import lax
from jax.experimental import pallas as pl
from jax.experimental.pallas import tpu as pltpu
from jax.sharding import PartitionSpec as P

L1, L2, HYPER, PROBES = 8192, 2048, 8, 8
ROWS, GRPS = 16, 8
LOCAL = L1 // ROWS
CH = 4
CR = LOCAL // CH
F32, BF16 = jnp.float32, jnp.bfloat16
MESH = pl.DeviceIdType.MESH
SCALE = 1.0 / (PROBES * L1 * L2)
NT = (((1,), (1,)), ((), ()))
NN = (((1,), (0,)), ((), ()))


def halves(table):
    hi = table.astype(ml_dtypes.bfloat16)
    lo = (table - hi.astype(np.float64)).astype(ml_dtypes.bfloat16)
    return hi, lo


@functools.lru_cache(maxsize=None)
def tables():
    x = np.arange(L2)
    w = np.zeros((8, 2, L2, 256), ml_dtypes.bfloat16)
    for pair in range(8):
        for t in range(2):
            j = (2 * pair + t) * 64 + np.arange(64)
            ang = 2 * math.pi * (x[:, None] * j[None, :] % L2) / L2
            hi, lo = halves(np.concatenate([np.cos(ang), -np.sin(ang)], 1))
            w[pair, 0, :, t * 128 : t * 128 + 128] = hi
            w[pair, 1, :, t * 128 : t * 128 + 128] = lo
    fh = np.arange(LOCAL)
    d = np.zeros((CH, 2, LOCAL, 2 * CR), ml_dtypes.bfloat16)
    for c in range(CH):
        r = c * CR + np.arange(CR)
        ang = 2 * math.pi * (fh[:, None] * r[None, :] % LOCAL) / LOCAL
        d[c, 0], d[c, 1] = halves(np.concatenate([np.cos(ang), np.sin(ang)], 1))
    r = np.arange(LOCAL)
    tw = np.zeros((LOCAL, 128), np.float32)
    for f in range(16):
        ang = 2 * math.pi * (r * f % L1) / L1
        tw[:, 2 * f], tw[:, 2 * f + 1] = np.cos(ang), np.sin(ang)
    tb = np.zeros((16, 64, 128), np.float32)
    for f in range(16):
        for dd in range(16):
            tb[f, 2 * dd] = math.cos(2 * math.pi * (dd * f % 16) / 16)
            tb[f, 2 * dd + 1] = math.sin(2 * math.pi * (dd * f % 16) / 16)
        for q in range(4):
            ang = 2 * math.pi * ((q * 128 + np.arange(128)) * f % L1) / L1
            for zu in range(2):
                tb[f, 32 + zu * 4 + q] = np.cos(ang)
                tb[f, 40 + zu * 4 + q] = np.sin(ang)
    return w, d, tw, tb


def split(v):
    hi = v.astype(BF16)
    return hi, (v - hi.astype(F32)).astype(BF16)


def mm(a, b, dims=NN):
    return lax.dot_general(a, b, dims, preferred_element_type=F32)


def exact(a, b):
    return lax.dot_general(a, b, NN, precision=lax.Precision.HIGHEST, preferred_element_type=F32)


def minus_i(v, sign):
    return pltpu.roll(v, 64, axis=1) * sign


def turn(v, m, sign):
    m = m % 16
    if m == 0:
        return v
    if m == 4:
        return minus_i(v, sign)
    return v * math.cos(2 * math.pi * m / 16) + minus_i(v, sign) * math.sin(2 * math.pi * m / 16)


def four(a, b, c, d, sign):
    s, t, u = a + c, a - c, b + d
    v = minus_i(b - d, sign)
    return s + u, t + v, s - u, t - v


def kernel(
    z_hbm, u_hbm, rs_hbm, cs_hbm, w_hbm, d_hbm, tw_hbm, tb_hbm,
    row_ref, col_ref,
    x, wbuf, dt, tw, tb, rs, cs, send, recv, acc, yh, yl, cross,
    bs, brecv, lb, upm, r32, tiles, mir, pex, qb, r1, q1, r2s, r2, q2s, q2,
    lsem, wsem, ssem, rsem, own, bss, brs, e1s, e1r, f1s, f1r, e2s, e2r, f2s, f2r,
):
    me, g = lax.axis_index("row"), lax.axis_index("grp")
    xh, y, core = me // 8, (me // 2) % 4, me % 2
    barrier = pltpu.get_barrier_semaphore()
    for k in range(1, ROWS):
        pl.semaphore_signal(barrier, inc=1, device_id={"row": lax.rem(me + k, ROWS)}, device_id_type=MESH)
    for k in range(1, GRPS):
        pl.semaphore_signal(barrier, inc=1, device_id={"grp": lax.rem(g + k, GRPS)}, device_id_type=MESH)

    def pair_of(s):
        o = s + 1
        return lax.rem(xh + lax.rem(o, 2), 2) * 4 + lax.rem(y + lax.rem(o // 2, 4), 4)

    def w_copy(s, slot):
        return pltpu.make_async_copy(w_hbm.at[pair_of(s)], wbuf.at[slot], wsem.at[slot])

    loads = [
        pltpu.make_async_copy(z_hbm.at[0], x.at[0], lsem.at[0]),
        pltpu.make_async_copy(u_hbm.at[0], x.at[1], lsem.at[1]),
        pltpu.make_async_copy(d_hbm, dt, lsem.at[2]),
        pltpu.make_async_copy(tw_hbm, tw, lsem.at[3]),
        pltpu.make_async_copy(tb_hbm.at[me], tb, lsem.at[4]),
        pltpu.make_async_copy(rs_hbm, rs, lsem.at[5]),
        pltpu.make_async_copy(cs_hbm, cs, lsem.at[6]),
    ]
    loads[0].start()
    w_copy(0, 0).start()
    for cp in loads[1:]:
        cp.start()

    def block(s, t, c):
        return pltpu.make_async_remote_copy(
            src_ref=send.at[s, t, c], dst_ref=recv.at[me, c], send_sem=ssem.at[c, 2 * s + t],
            recv_sem=rsem.at[c, me], device_id={"row": 2 * pair_of(s) + t}, device_id_type=MESH,
        )

    def arrival(c, d):
        return pltpu.make_async_remote_copy(
            src_ref=send.at[0, 0, c], dst_ref=recv.at[d, c], send_sem=ssem.at[c, 0],
            recv_sem=rsem.at[c, d], device_id={"row": d}, device_id_type=MESH,
        )

    def start_block(s, c):
        @pl.when(s < 7)
        def _():
            block(s, 0, c).start()
            block(s, 1, c).start()

        @pl.when(s == 7)
        def _():
            block(7, 1 - core, c).start()

    loads[0].wait()
    loads[1].wait()
    pl.semaphore_wait(barrier, ROWS - 1 + GRPS - 1)

    def section(s, _):
        slot = lax.rem(s, 2)
        w_copy(s, slot).wait()

        @pl.when(s < 7)
        def _():
            w_copy(s + 1, 1 - slot).start()

        for zu in range(2):
            got = mm(x[zu], wbuf[slot, 0]) + mm(x[zu], wbuf[slot, 1])
            for t in range(2):
                for c in range(CH):
                    send[s, t, c, pl.ds(zu * CR, CR)] = got[c * CR : (c + 1) * CR, t * 128 : (t + 1) * 128]
        start_block(s, 0)
        return 0

    lax.fori_loop(0, 8, section, 0)
    mine = pltpu.make_async_copy(send.at[7, core], recv.at[me], own)
    mine.start()

    lane = lax.broadcasted_iota(jnp.int32, (8, 128), 1)
    sub = lax.broadcasted_iota(jnp.int32, (128, 128), 0)
    lan = lax.broadcasted_iota(jnp.int32, (128, 128), 1)
    parity = lax.broadcasted_iota(jnp.int32, (L2, 128), 0) % 2
    alt = (1 - 2 * parity).astype(F32).astype(BF16)
    for zu in range(2):
        summed = mm(x[zu], alt)
        for q in range(4):
            bs[pl.ds(zu * 4 + q, 1)] = jnp.sum(
                jnp.where(sub == lan, summed[q * 128 : (q + 1) * 128], 0.0), axis=0, keepdims=True
            )

    def b_copy(k):
        return pltpu.make_async_remote_copy(
            src_ref=bs, dst_ref=brecv.at[me], send_sem=bss.at[k], recv_sem=brs.at[me],
            device_id={"row": lax.rem(me + k, ROWS)}, device_id_type=MESH,
        )

    for k in range(1, ROWS):
        b_copy(k).start()
    for c in range(1, CH):
        lax.fori_loop(0, 8, lambda s, _, c=c: (start_block(s, c), 0)[1], 0)

    for cp in loads[2:]:
        cp.wait()
    flip = (lax.rem(sub + lan, 128) == 0).astype(F32)

    def stack_r(t, _):
        tiles[t] = rs[:, pl.ds(pl.multiple_of(t * 128, 128), 128)]
        return 0

    lax.fori_loop(0, 64, stack_r, 0)
    mir[...] = exact(tiles[...].reshape(512, 128), flip).reshape(64, 8, 128)

    def put_r(t, _):
        back = jnp.where(lane == 0, mir[lax.rem(64 - t, 64)], mir[63 - t])
        both = jnp.concatenate([tiles[t], back], axis=0)
        hi, lo = split(both)
        at = pl.ds(pl.multiple_of(t * 128, 128), 128)
        r32[pl.ds(0, 16), at] = hi
        r32[pl.ds(16, 16), at] = lo
        return 0

    lax.fori_loop(0, 64, put_r, 0)

    def own_half(tile):
        other = pltpu.roll(tile, 64, axis=1)
        low = lane < 64
        return jnp.where(core == 0, jnp.where(low, tile, other), jnp.where(low, other, tile))

    at = me // 2
    c_here = cs[:, pl.ds(pl.multiple_of(at * 128, 128), 128)]
    c_a = cs[:, pl.ds(pl.multiple_of((15 - at) * 128, 128), 128)]
    c_b = cs[:, pl.ds(pl.multiple_of(lax.rem(16 - at, 16) * 128, 128), 128)]
    c_back = jnp.where(lane == 0, exact(c_b, flip), exact(c_a, flip))
    c_back = own_half(c_back)
    c_back = jnp.where(jnp.logical_and(me == 0, lax.rem(lane, 64) == 0), 0.0, c_back)
    c_hi, c_lo = split(jnp.concatenate([own_half(c_here), c_back], axis=0))
    c_both = jnp.concatenate([c_hi, c_lo], axis=0)

    for k in range(1, ROWS):
        d = lax.rem(me + k, ROWS)
        pltpu.make_async_remote_copy(
            src_ref=bs, dst_ref=brecv.at[d], send_sem=bss.at[0], recv_sem=brs.at[d],
            device_id={"row": d}, device_id_type=MESH,
        ).wait_recv()
    brecv[me] = bs[...]
    re = jnp.zeros((8, 128), F32)
    im = jnp.zeros((8, 128), F32)
    for d in range(ROWS):
        re = re + brecv[d] * tb[pl.ds(2 * d, 1)]
        im = im - brecv[d] * tb[pl.ds(2 * d + 1, 1)]
    tc, ts = tb[pl.ds(32, 8)], tb[pl.ds(40, 8)]
    bs2_re = re * tc + im * ts
    bs2_im = im * tc - re * ts
    lb[...] = jnp.zeros_like(lb)
    for q in range(4):
        for zu in range(2):
            a = bs2_re[zu * 4 + q : zu * 4 + q + 1]
            b = bs2_im[zu * 4 + q : zu * 4 + q + 1]
            lb[pl.ds(zu, 1), pl.ds(q * 256, 128)] = a
            lb[pl.ds(zu, 1), pl.ds(q * 256 + 128, 128)] = b
            lb[pl.ds(2 + zu, 1), pl.ds(q * 256, 128)] = b
            lb[pl.ds(2 + zu, 1), pl.ds(q * 256 + 128, 128)] = -a
    mid = jnp.zeros((16, LOCAL), F32)
    for q in range(4):
        hi, lo = split(lb[:, q * 256 : (q + 1) * 256])
        mid = mid + mm(hi, dt[q, 0], NT) + mm(lo, dt[q, 0], NT) + mm(hi, dt[q, 1], NT)
    mid_cross = mid[0:1] * mid[1:2] + mid[2:3] * mid[3:4]
    lb[...] = jnp.zeros_like(lb)
    for q in range(4):
        lb[pl.ds(q, 1), pl.ds(0, 128)] = mid_cross[:, q * 128 : (q + 1) * 128]
    spread = (
        lax.broadcasted_iota(jnp.int32, (128, 2048), 1) == 16 * lax.broadcasted_iota(jnp.int32, (128, 2048), 0) + me
    ).astype(F32)
    upm[...] = exact(lb[pl.ds(0, 8), pl.ds(0, 128)], spread)
    c_mid = jnp.broadcast_to(cs[:, 1024:1025], (8, 128))
    total = jnp.zeros((8, 128), F32)
    for q in range(4):

        def put_mid(t, total, q=q):
            up = upm[pl.ds(q, 1), pl.ds(pl.multiple_of(t * 128, 128), 128)]
            pex[q * 16 + t] = c_mid * up
            return total + tiles[q * 16 + t] * up

        total = lax.fori_loop(0, 16, put_mid, total)
    qb[pl.ds(16, 8)] = jnp.broadcast_to(jnp.sum(total, axis=1, keepdims=True), (8, 128))

    sign = jnp.where(lax.broadcasted_iota(jnp.int32, (16, 128), 1) < 64, 1.0, -1.0).astype(F32)
    mine.wait()

    def turned(c):
        for k in range(1, ROWS):
            arrival(c, lax.rem(me + k, ROWS)).wait_recv()

        def rows16(i, _):
            at = pl.ds(pl.multiple_of(i * 16, 16), 16)
            jat = pl.ds(pl.multiple_of(CR + i * 16, 16), 16)
            coef = tw[pl.ds(pl.multiple_of(c * CR + i * 16, 16), 16)]
            for zu in range(2):
                v = [recv[d, c, pl.ds(pl.multiple_of(zu * CR + i * 16, 16), 16)] for d in range(ROWS)]
                inner = [four(v[d0], v[d0 + 4], v[d0 + 8], v[d0 + 12], sign) for d0 in range(4)]
                for f0 in range(4):
                    outs = four(*[turn(inner[d0][f0], d0 * f0, sign) for d0 in range(4)], sign)
                    for f1 in range(4):
                        f = f0 + 4 * f1
                        val = outs[f1]
                        jval = minus_i(val, sign)
                        if f:
                            cc = jnp.broadcast_to(coef[:, 2 * f : 2 * f + 1], (16, 128))
                            ss = jnp.broadcast_to(coef[:, 2 * f + 1 : 2 * f + 2], (16, 128))
                            val, jval = val * cc + jval * ss, jval * cc - val * ss
                        cols = pl.ds(f * 256 + zu * 128, 128)
                        yh[at, cols], yl[at, cols] = split(val)
                        yh[jat, cols], yl[jat, cols] = split(jval)
            return 0

        lax.fori_loop(0, CR // 16, rows16, 0)

    def product(c, cols):
        a, b = yh[:, cols], yl[:, cols]
        return mm(dt[c, 0], a) + mm(dt[c, 0], b) + mm(dt[c, 1], a)

    for c in range(CH - 1):
        turned(c)

        def add(n, _, c=c):
            cols = pl.ds(pl.multiple_of(n * 512, 512), 512)
            got = product(c, cols)
            acc[:, cols] = got if c == 0 else acc[:, cols] + got
            return 0

        lax.fori_loop(0, 8, add, 0)

    turned(CH - 1)

    def finish(n, _):
        cols = pl.ds(pl.multiple_of(n * 512, 512), 512)
        got = acc[:, cols] + product(CH - 1, cols)
        for h in range(2):
            cross[pl.ds(2 * n + h, LOCAL, stride=16)] = (
                got[:, h * 256 : h * 256 + 128] * got[:, h * 256 + 128 : h * 256 + 256]
            )
        return 0

    lax.fori_loop(0, 8, finish, 0)

    def contract(n, q):
        at = pl.ds(pl.multiple_of(n * 512, 512), 512)
        hi, lo = split(cross[at])
        a = mm(c_both, hi, NT)
        p = a[:16] + a[16:] + mm(c_hi, lo, NT)
        for i in range(4):
            pex[n * 4 + i] = pex[n * 4 + i] + p[:8, i * 128 : (i + 1) * 128]
            tiles[n * 4 + i] = p[8:, i * 128 : (i + 1) * 128]
        weights = r32[:, at]
        b = mm(weights, hi)
        return q + b[:16] + b[16:] + mm(weights[:16], lo)

    qb[pl.ds(0, 16)] = lax.fori_loop(0, 16, contract, jnp.zeros((16, 128), F32))
    mir[...] = exact(tiles[...].reshape(512, 128), flip).reshape(64, 8, 128)

    def join(t, _):
        back = jnp.where(lane == 0, mir[lax.rem(64 - t, 64)], mir[63 - t])
        pex[t] = (pex[t] + back) * SCALE
        return 0

    lax.fori_loop(0, 64, join, 0)
    qb[...] = qb[...] * SCALE

    def grp_copies(k):
        to = lax.rem(g + k, GRPS)
        return (
            pltpu.make_async_remote_copy(
                src_ref=pex.at[pl.ds(to * 8, 8)], dst_ref=r1.at[g], send_sem=e1s.at[k], recv_sem=e1r.at[g],
                device_id={"grp": to}, device_id_type=MESH,
            ),
            pltpu.make_async_remote_copy(
                src_ref=qb, dst_ref=q1.at[g], send_sem=f1s.at[k], recv_sem=f1r.at[g],
                device_id={"grp": to}, device_id_type=MESH,
            ),
        )

    def grp_arrivals(k):
        d = lax.rem(g + k, GRPS)
        return (
            pltpu.make_async_remote_copy(
                src_ref=pex.at[pl.ds(0, 8)], dst_ref=r1.at[d], send_sem=e1s.at[0], recv_sem=e1r.at[d],
                device_id={"grp": d}, device_id_type=MESH,
            ),
            pltpu.make_async_remote_copy(
                src_ref=qb, dst_ref=q1.at[d], send_sem=f1s.at[0], recv_sem=f1r.at[d],
                device_id={"grp": d}, device_id_type=MESH,
            ),
        )

    for k in range(1, GRPS):
        for cp in grp_copies(k):
            cp.start()
    r1[g] = pex[pl.ds(g * 8, 8)]
    q1[g] = qb[...]
    for k in range(1, GRPS):
        for cp in grp_arrivals(k):
            cp.wait_recv()
    r2s[...] = functools.reduce(lambda a, d: a + r1[d], range(1, GRPS), r1[0])
    q2s[...] = functools.reduce(lambda a, d: a + q1[d], range(1, GRPS), q1[0])

    def row_copies(k):
        to = lax.rem(me + k, ROWS)
        return (
            pltpu.make_async_remote_copy(
                src_ref=r2s.at[to // 2], dst_ref=r2.at[me], send_sem=e2s.at[k], recv_sem=e2r.at[me],
                device_id={"row": to}, device_id_type=MESH,
            ),
            pltpu.make_async_remote_copy(
                src_ref=q2s, dst_ref=q2.at[me], send_sem=f2s.at[k], recv_sem=f2r.at[me],
                device_id={"row": to}, device_id_type=MESH,
            ),
        )

    def row_arrivals(k):
        d = lax.rem(me + k, ROWS)
        return (
            pltpu.make_async_remote_copy(
                src_ref=r2s.at[0], dst_ref=r2.at[d], send_sem=e2s.at[0], recv_sem=e2r.at[d],
                device_id={"row": d}, device_id_type=MESH,
            ),
            pltpu.make_async_remote_copy(
                src_ref=q2s, dst_ref=q2.at[d], send_sem=f2s.at[0], recv_sem=f2r.at[d],
                device_id={"row": d}, device_id_type=MESH,
            ),
        )

    for k in range(1, ROWS):
        for cp in row_copies(k):
            cp.start()
    r2[me] = r2s[me // 2]
    q2[me] = q2s[...]
    for k in range(1, ROWS):
        for cp in row_arrivals(k):
            cp.wait_recv()
    tile = functools.reduce(lambda a, d: a + r2[d], range(1, ROWS), r2[0])
    row_ref[...] = jnp.where(core == 0, tile, pltpu.roll(tile, 64, axis=1))[:, :64]
    low = lax.broadcasted_iota(jnp.int32, (16, 128), 1) < 64
    middle = functools.reduce(lambda a, d: a + q2[d, pl.ds(16, 8)], range(1, ROWS), q2[0, pl.ds(16, 8)])
    for m in range(8):
        a, b = q2[2 * m, pl.ds(0, 16)], q2[2 * m + 1, pl.ds(0, 16)]
        ab = jnp.where(low, a + pltpu.roll(a, 64, axis=1), b + pltpu.roll(b, 64, axis=1))
        col_ref[:, pl.ds(m * 128, 128)] = ab[:8]
        tiles[m] = ab[8:]
    mir[pl.ds(0, 8)] = exact(tiles[pl.ds(0, 8)].reshape(64, 128), flip).reshape(8, 8, 128)
    for t in range(8, 16):
        first = middle if t == 8 else mir[16 - t]
        col_ref[:, pl.ds(t * 128, 128)] = jnp.where(lane == 0, first, mir[15 - t])

    for c in range(CH):

        def drain(s, _, c=c):
            @pl.when(s < 7)
            def _():
                block(s, 0, c).wait_send()
                block(s, 1, c).wait_send()

            @pl.when(s == 7)
            def _():
                block(7, 1 - core, c).wait_send()

            return 0

        lax.fori_loop(0, 8, drain, 0)
    for k in range(1, ROWS):
        b_copy(k).wait_send()
        for cp in row_copies(k):
            cp.wait_send()
    for k in range(1, GRPS):
        for cp in grp_copies(k):
            cp.wait_send()


def local(probes, solves, row_spectra, col_spectra):
    w, d, tw, tb = (jnp.asarray(t) for t in tables())
    dma = pltpu.SemaphoreType.DMA
    vm = pltpu.VMEM
    scratch = [
        vm((2, LOCAL, L2), BF16), vm((2, 2, L2, 256), BF16), vm((CH, 2, LOCAL, 2 * CR), BF16),
        vm((LOCAL, 128), F32), vm((64, 128), F32), vm((8, L1), F32), vm((8, L2), F32),
        vm((8, 2, CH, 2 * CR, 128), F32), vm((ROWS, CH, 2 * CR, 128), F32),
        vm((LOCAL, 4096), F32), vm((2 * CR, 4096), BF16), vm((2 * CR, 4096), BF16), vm((L1, 128), F32),
        vm((8, 128), F32), vm((ROWS, 8, 128), F32), vm((16, 1024), F32), vm((8, 2048), F32),
        vm((32, L1), BF16), vm((64, 8, 128), F32), vm((64, 8, 128), F32), vm((64, 8, 128), F32), vm((24, 128), F32),
        vm((GRPS, 8, 8, 128), F32), vm((GRPS, 24, 128), F32), vm((8, 8, 128), F32), vm((ROWS, 8, 128), F32),
        vm((24, 128), F32), vm((ROWS, 24, 128), F32),
        dma((7,)), dma((2,)), dma((CH, ROWS)), dma((CH, ROWS)), dma, dma((ROWS,)), dma((ROWS,)),
        dma((GRPS,)), dma((GRPS,)), dma((GRPS,)), dma((GRPS,)),
        dma((ROWS,)), dma((ROWS,)), dma((ROWS,)), dma((ROWS,)),
    ]
    hbm = pl.BlockSpec(memory_space=pl.ANY)
    return pl.pallas_call(
        kernel,
        out_shape=(jax.ShapeDtypeStruct((HYPER, 64), F32), jax.ShapeDtypeStruct((HYPER, L2), F32)),
        in_specs=[hbm] * 8,
        out_specs=(pl.BlockSpec(memory_space=pltpu.VMEM), pl.BlockSpec(memory_space=pltpu.VMEM)),
        scratch_shapes=scratch,
        compiler_params=pltpu.CompilerParams(collective_id=0, has_side_effects=True, vmem_limit_bytes=62 << 20),
        name="trace_terms",
    )(probes, solves, row_spectra, col_spectra, w, d, tw, tb)


def solution(mesh):
    placed = (P("grp", "row", None), P("grp", "row", None), P(), P())
    return jax.shard_map(
        local, mesh=mesh, in_specs=placed, out_specs=(P(None, ("grp", "row")), P()), check_vma=False
    )
```

```python
import functools
import math

import jax
import jax.numpy as jnp
import ml_dtypes
import numpy as np
from jax import lax
from jax.experimental import pallas as pl
from jax.experimental.pallas import tpu as pltpu
from jax.sharding import PartitionSpec as P

L1, L2, HYPER, PROBES = 8192, 2048, 8, 8
ROWS, GRPS = 16, 8
LOCAL = L1 // ROWS
SIZES = (128, 128, 128, 64, 32, 32)
STARTS = tuple(sum(SIZES[:c]) for c in range(len(SIZES)))
CH = len(SIZES)
WIDTHS = tuple((6 if n == 128 else 8) * n for n in SIZES) + (512,)
OFFS = tuple(sum(WIDTHS[:c]) for c in range(len(WIDTHS)))
F32, BF16 = jnp.float32, jnp.bfloat16
MESH = pl.DeviceIdType.MESH
SCALE = 1.0 / (PROBES * L1 * L2)
NT = (((1,), (1,)), ((), ()))
NN = (((1,), (0,)), ((), ()))


def halves(table):
    hi = table.astype(ml_dtypes.bfloat16)
    lo = (table - hi.astype(np.float64)).astype(ml_dtypes.bfloat16)
    return hi, lo


@functools.lru_cache(maxsize=None)
def tables():
    x = np.arange(L2)
    w = np.zeros((8, 2, L2, 256), ml_dtypes.bfloat16)
    for pair in range(8):
        for t in range(2):
            j = (2 * pair + t) * 64 + np.arange(64)
            ang = 2 * math.pi * (x[:, None] * j[None, :] % L2) / L2
            hi, lo = halves(np.concatenate([np.cos(ang), -np.sin(ang)], 1))
            w[pair, 0, :, t * 128 : t * 128 + 128] = hi
            w[pair, 1, :, t * 128 : t * 128 + 128] = lo
    fh = np.arange(LOCAL)
    d = np.zeros((LOCAL, sum(WIDTHS)), ml_dtypes.bfloat16)
    for c, (first, n) in enumerate(zip(STARTS + (384,), SIZES + (128,))):
        r = first + np.arange(n)
        ang = 2 * math.pi * (fh[:, None] * r[None, :] % LOCAL) / LOCAL
        hi, lo = halves(np.concatenate([np.cos(ang), np.sin(ang)], 1))
        parts = [hi, lo] if c == CH else [hi, hi, lo] if n == 128 else [hi, hi, lo, lo]
        d[:, OFFS[c] : OFFS[c] + WIDTHS[c]] = np.concatenate(parts, 1)
    r = np.arange(LOCAL)
    tw = np.zeros((LOCAL, 128), np.float32)
    for f in range(16):
        ang = 2 * math.pi * (r * f % L1) / L1
        tw[:, 2 * f], tw[:, 2 * f + 1] = np.cos(ang), np.sin(ang)
    tb = np.zeros((16, 64, 128), np.float32)
    for f in range(16):
        for dd in range(16):
            tb[f, 2 * dd] = math.cos(2 * math.pi * (dd * f % 16) / 16)
            tb[f, 2 * dd + 1] = math.sin(2 * math.pi * (dd * f % 16) / 16)
        for q in range(4):
            ang = 2 * math.pi * ((q * 128 + np.arange(128)) * f % L1) / L1
            for zu in range(2):
                tb[f, 32 + zu * 4 + q] = np.cos(ang)
                tb[f, 40 + zu * 4 + q] = np.sin(ang)
    return w, d, tw, tb


def split(v):
    hi = v.astype(BF16)
    return hi, (v - hi.astype(F32)).astype(BF16)


def mm(a, b, dims=NN):
    return lax.dot_general(a, b, dims, preferred_element_type=F32)


def exact(a, b):
    return lax.dot_general(a, b, NN, precision=lax.Precision.HIGHEST, preferred_element_type=F32)


def minus_i(v, sign):
    return pltpu.roll(v, 64, axis=1) * sign


def turn(v, m, sign):
    m = m % 16
    if m == 0:
        return v
    if m == 4:
        return minus_i(v, sign)
    return v * math.cos(2 * math.pi * m / 16) + minus_i(v, sign) * math.sin(2 * math.pi * m / 16)


def four(a, b, c, d, sign):
    s, t, u = a + c, a - c, b + d
    v = minus_i(b - d, sign)
    return s + u, t + v, s - u, t - v


def kernel(
    z_hbm, u_hbm, rs_hbm, cs_hbm, w_hbm, d_hbm, tw_hbm, tb_hbm,
    row_ref, col_ref,
    x, wbuf, dt, tw, tb, rs, cs, send, recv, acc, yy, cross,
    bs, brecv, ms, mrecv, lb, upm, r32, tiles, mir, pex, qb, r1, q1, r2s, r2, q2s, q2,
    lsem, wsem, ssem, rsem, own, bss, brs, mss, mrs, e1s, e1r, f1s, f1r, e2s, e2r, f2s, f2r,
):
    me, g = lax.axis_index("row"), lax.axis_index("grp")
    xh, y, core = me // 8, (me // 2) % 4, me % 2
    barrier = pltpu.get_barrier_semaphore()
    for k in range(1, ROWS):
        pl.semaphore_signal(barrier, inc=1, device_id={"row": lax.rem(me + k, ROWS)}, device_id_type=MESH)
    for k in range(1, GRPS):
        pl.semaphore_signal(barrier, inc=1, device_id={"grp": lax.rem(g + k, GRPS)}, device_id_type=MESH)

    def pair_of(s):
        m = s % 4
        dy = (2 + 3 * m + 3 * (m * (m - 1) // 2)) % 4
        return lax.rem(xh + 1 - s // 4, 2) * 4 + lax.rem(y + dy, 4)

    def w_copy(s, slot):
        return pltpu.make_async_copy(w_hbm.at[pair_of(s)], wbuf.at[slot], wsem.at[slot])

    loads = [
        pltpu.make_async_copy(z_hbm.at[0], x.at[0], lsem.at[0]),
        pltpu.make_async_copy(u_hbm.at[0], x.at[1], lsem.at[1]),
        pltpu.make_async_copy(d_hbm, dt, lsem.at[2]),
        pltpu.make_async_copy(tw_hbm, tw, lsem.at[3]),
        pltpu.make_async_copy(tb_hbm.at[me], tb, lsem.at[4]),
        pltpu.make_async_copy(rs_hbm, rs, lsem.at[5]),
        pltpu.make_async_copy(cs_hbm, cs, lsem.at[6]),
    ]
    loads[0].start()
    w_copy(0, 0).start()
    loads[1].start()

    def span(c):
        return pl.ds(2 * STARTS[c], 2 * SIZES[c])

    def block(s, t, c):
        return pltpu.make_async_remote_copy(
            src_ref=send.at[s, t, span(c)], dst_ref=recv.at[me, span(c)], send_sem=ssem.at[c, 2 * s + t],
            recv_sem=rsem.at[c, me], device_id={"row": 2 * pair_of(s) + t}, device_id_type=MESH,
        )

    def arrival(c, d):
        return pltpu.make_async_remote_copy(
            src_ref=send.at[0, 0, span(c)], dst_ref=recv.at[d, span(c)], send_sem=ssem.at[c, 0],
            recv_sem=rsem.at[c, d], device_id={"row": d}, device_id_type=MESH,
        )

    def start_block(s, c):
        @pl.when(s < 7)
        def _():
            block(s, 0, c).start()
            block(s, 1, c).start()

        @pl.when(s == 7)
        def _():
            block(7, 1 - core, c).start()

    loads[0].wait()
    loads[1].wait()
    pl.semaphore_wait(barrier, ROWS - 1 + GRPS - 1)

    def section(s, _):
        slot = lax.rem(s, 2)
        w_copy(s, slot).wait()

        @pl.when(s < 7)
        def _():
            w_copy(s + 1, 1 - slot).start()

        for zu in range(2):
            got = mm(x[zu], wbuf[slot, 0]) + mm(x[zu], wbuf[slot, 1])
            for t in range(2):
                for c in range(CH):
                    first, n = STARTS[c], SIZES[c]
                    send[s, t, pl.ds(2 * first + zu * n, n)] = got[first : first + n, t * 128 : (t + 1) * 128]
        start_block(s, 0)
        return 0

    lax.fori_loop(0, 8, section, 0)
    for cp in loads[2:]:
        cp.start()
    mine = pltpu.make_async_copy(send.at[7, core], recv.at[me], own)
    mine.start()

    lane = lax.broadcasted_iota(jnp.int32, (8, 128), 1)
    sub = lax.broadcasted_iota(jnp.int32, (128, 128), 0)
    lan = lax.broadcasted_iota(jnp.int32, (128, 128), 1)
    parity = lax.broadcasted_iota(jnp.int32, (L2, 128), 0) % 2
    alt = (1 - 2 * parity).astype(F32).astype(BF16)
    for zu in range(2):
        summed = mm(x[zu], alt)
        for q in range(4):
            bs[pl.ds(zu * 4 + q, 1)] = jnp.sum(
                jnp.where(sub == lan, summed[q * 128 : (q + 1) * 128], 0.0), axis=0, keepdims=True
            )

    def b_copy(k):
        return pltpu.make_async_remote_copy(
            src_ref=bs, dst_ref=brecv.at[me], send_sem=bss.at[k], recv_sem=brs.at[me],
            device_id={"row": lax.rem(me + k, ROWS)}, device_id_type=MESH,
        )

    for k in range(1, ROWS):
        b_copy(k).start()
    for c in range(1, CH):
        lax.fori_loop(0, 8, lambda s, _, c=c: (start_block(s, c), 0)[1], 0)

    for cp in loads[2:]:
        cp.wait()
    flip = (lax.rem(sub + lan, 128) == 0).astype(F32)

    def stack_r(t, _):
        tiles[t] = rs[:, pl.ds(pl.multiple_of(t * 128, 128), 128)]
        return 0

    lax.fori_loop(0, 64, stack_r, 0)
    mir[...] = exact(tiles[...].reshape(512, 128), flip).reshape(64, 8, 128)

    def put_r(t, _):
        back = jnp.where(lane == 0, mir[lax.rem(64 - t, 64)], mir[63 - t])
        both = jnp.concatenate([tiles[t], back], axis=0)
        hi, lo = split(both)
        at = pl.ds(pl.multiple_of(t * 128, 128), 128)
        r32[pl.ds(0, 16), at] = hi
        r32[pl.ds(16, 16), at] = lo
        return 0

    lax.fori_loop(0, 64, put_r, 0)

    def own_half(tile):
        other = pltpu.roll(tile, 64, axis=1)
        low = lane < 64
        return jnp.where(core == 0, jnp.where(low, tile, other), jnp.where(low, other, tile))

    at = me // 2
    c_here = cs[:, pl.ds(pl.multiple_of(at * 128, 128), 128)]
    c_a = cs[:, pl.ds(pl.multiple_of((15 - at) * 128, 128), 128)]
    c_b = cs[:, pl.ds(pl.multiple_of(lax.rem(16 - at, 16) * 128, 128), 128)]
    c_back = jnp.where(lane == 0, exact(c_b, flip), exact(c_a, flip))
    c_back = own_half(c_back)
    c_back = jnp.where(jnp.logical_and(me == 0, lax.rem(lane, 64) == 0), 0.0, c_back)
    c_hi, c_lo = split(jnp.concatenate([own_half(c_here), c_back], axis=0))
    c_both = jnp.concatenate([c_hi, c_lo], axis=0)

    for k in range(1, ROWS):
        d = lax.rem(me + k, ROWS)
        pltpu.make_async_remote_copy(
            src_ref=bs, dst_ref=brecv.at[d], send_sem=bss.at[0], recv_sem=brs.at[d],
            device_id={"row": d}, device_id_type=MESH,
        ).wait_recv()
    brecv[me] = bs[...]
    re = jnp.zeros((8, 128), F32)
    im = jnp.zeros((8, 128), F32)
    for d in range(ROWS):
        re = re + brecv[d] * tb[pl.ds(2 * d, 1)]
        im = im - brecv[d] * tb[pl.ds(2 * d + 1, 1)]
    tc, ts = tb[pl.ds(32, 8)], tb[pl.ds(40, 8)]
    bs2_re = re * tc + im * ts
    bs2_im = im * tc - re * ts
    lb[...] = jnp.zeros_like(lb)
    for q in range(4):
        for zu in range(2):
            a = bs2_re[zu * 4 + q : zu * 4 + q + 1]
            b = bs2_im[zu * 4 + q : zu * 4 + q + 1]
            lb[pl.ds(zu, 1), pl.ds(q * 256, 128)] = a
            lb[pl.ds(zu, 1), pl.ds(q * 256 + 128, 128)] = b
            lb[pl.ds(2 + zu, 1), pl.ds(q * 256, 128)] = b
            lb[pl.ds(2 + zu, 1), pl.ds(q * 256 + 128, 128)] = -a
    mid = jnp.zeros((16, LOCAL), F32)
    for q in range(4):
        hi, lo = split(lb[:, q * 256 : (q + 1) * 256])
        at = OFFS[q] if q < 3 else OFFS[CH]
        d_hi = dt[:, at : at + 256]
        d_lo = dt[:, at + WIDTHS[q if q < 3 else CH] - 256 : at + WIDTHS[q if q < 3 else CH]]
        mid = mid + mm(hi, d_hi, NT) + mm(lo, d_hi, NT) + mm(hi, d_lo, NT)
    mid_cross = mid[0:1] * mid[1:2] + mid[2:3] * mid[3:4]
    lb[...] = jnp.zeros_like(lb)
    for q in range(4):
        lb[pl.ds(q, 1), pl.ds(0, 128)] = mid_cross[:, q * 128 : (q + 1) * 128]
    spread = (
        lax.broadcasted_iota(jnp.int32, (128, 2048), 1) == 16 * lax.broadcasted_iota(jnp.int32, (128, 2048), 0) + me
    ).astype(F32)
    upm[...] = exact(lb[pl.ds(0, 8), pl.ds(0, 128)], spread)
    c_mid = jnp.broadcast_to(cs[:, 1024:1025], (8, 128))
    total = jnp.zeros((8, 128), F32)
    for q in range(4):

        def put_mid(t, total, q=q):
            up = upm[pl.ds(q, 1), pl.ds(pl.multiple_of(t * 128, 128), 128)]
            pex[q * 16 + t] = c_mid * up
            return total + tiles[q * 16 + t] * up

        total = lax.fori_loop(0, 16, put_mid, total)
    ms[...] = jnp.broadcast_to(jnp.sum(total, axis=1, keepdims=True), (8, 128))

    def m_copy(k):
        return pltpu.make_async_remote_copy(
            src_ref=ms, dst_ref=mrecv.at[me], send_sem=mss.at[k], recv_sem=mrs.at[me],
            device_id={"row": lax.rem(me + k, ROWS)}, device_id_type=MESH,
        )

    for k in range(1, ROWS):
        m_copy(k).start()
    mrecv[me] = ms[...]

    sign = jnp.where(lax.broadcasted_iota(jnp.int32, (16, 128), 1) < 64, 1.0, -1.0).astype(F32)
    mine.wait()

    def turned(c):
        for k in range(1, ROWS):
            arrival(c, lax.rem(me + k, ROWS)).wait_recv()

        n = SIZES[c]

        def rows16(i, _):
            ats = [pl.ds(pl.multiple_of(2 * n * p + i * 16, 16), 16) for p in range(2 if n == 128 else 4)]
            jats = [pl.ds(pl.multiple_of(2 * n * p + n + i * 16, 16), 16) for p in range(2 if n == 128 else 4)]
            coef = tw[pl.ds(pl.multiple_of(STARTS[c] + i * 16, 16), 16)]
            for zu in range(2):
                at = pl.ds(pl.multiple_of(2 * STARTS[c] + zu * n + i * 16, 16), 16)
                v = [recv[d, at] for d in range(ROWS)]
                inner = [four(v[d0], v[d0 + 4], v[d0 + 8], v[d0 + 12], sign) for d0 in range(4)]
                for f0 in range(4):
                    outs = four(*[turn(inner[d0][f0], d0 * f0, sign) for d0 in range(4)], sign)
                    for f1 in range(4):
                        f = f0 + 4 * f1
                        val = outs[f1]
                        jval = minus_i(val, sign)
                        if f:
                            cc = jnp.broadcast_to(coef[:, 2 * f : 2 * f + 1], (16, 128))
                            ss = jnp.broadcast_to(coef[:, 2 * f + 1 : 2 * f + 2], (16, 128))
                            val, jval = val * cc + jval * ss, jval * cc - val * ss
                        cols = pl.ds(f * 256 + zu * 128, 128)
                        for p, (part, jpart) in enumerate(zip(split(val), split(jval))):
                            for copy in range(p, len(ats), 2):
                                yy[ats[copy], cols] = part
                                yy[jats[copy], cols] = jpart
            return 0

        lax.fori_loop(0, n // 16, rows16, 0)

    def product(c, cols):
        at, n = OFFS[c], SIZES[c]
        if n == 128:
            return mm(dt[:, at : at + 512], yy[pl.ds(0, 512), cols]) + mm(dt[:, at + 512 : at + 768], yy[pl.ds(0, 256), cols])
        return mm(dt[:, at : at + 8 * n], yy[pl.ds(0, 8 * n), cols])

    for c in range(CH - 1):
        turned(c)

        def add(n, _, c=c):
            cols = pl.ds(pl.multiple_of(n * 512, 512), 512)
            got = product(c, cols)
            acc[:, cols] = got if c == 0 else acc[:, cols] + got
            return 0

        lax.fori_loop(0, 8, add, 0)
    for k in range(1, ROWS):
        d = lax.rem(me + k, ROWS)
        pltpu.make_async_remote_copy(
            src_ref=ms, dst_ref=mrecv.at[d], send_sem=mss.at[0], recv_sem=mrs.at[d],
            device_id={"row": d}, device_id_type=MESH,
        ).wait_recv()
    middle = functools.reduce(lambda a, d: a + mrecv[d], range(1, ROWS), mrecv[0])

    turned(CH - 1)

    def finish(n, _):
        cols = pl.ds(pl.multiple_of(n * 512, 512), 512)
        got = acc[:, cols] + product(CH - 1, cols)
        for h in range(2):
            cross[pl.ds(2 * n + h, LOCAL, stride=16)] = (
                got[:, h * 256 : h * 256 + 128] * got[:, h * 256 + 128 : h * 256 + 256]
            )
        return 0

    lax.fori_loop(0, 8, finish, 0)

    def contract(n, q):
        at = pl.ds(pl.multiple_of(n * 512, 512), 512)
        hi, lo = split(cross[at])
        a = mm(c_both, hi, NT)
        p = a[:16] + a[16:] + mm(c_hi, lo, NT)
        for i in range(4):
            pex[n * 4 + i] = pex[n * 4 + i] + p[:8, i * 128 : (i + 1) * 128]
            tiles[n * 4 + i] = p[8:, i * 128 : (i + 1) * 128]
        weights = r32[:, at]
        b = mm(weights, hi)
        return q + b[:16] + b[16:] + mm(weights[:16], lo)

    q = lax.fori_loop(0, 16, contract, jnp.zeros((16, 128), F32), unroll=4)
    q = q + pltpu.roll(q, 64, axis=1)
    q = jnp.where(lane < 64, q[:8], q[8:])
    qb[...] = jnp.where(jnp.logical_and(me == 0, lane == 64), middle, q) * SCALE
    mir[...] = exact(tiles[...].reshape(512, 128), flip).reshape(64, 8, 128)

    def join(t, _):
        back = jnp.where(lane == 0, mir[lax.rem(64 - t, 64)], mir[63 - t])
        pex[t] = (pex[t] + back) * SCALE
        return 0

    lax.fori_loop(0, 64, join, 0, unroll=8)

    def grp_copies(k):
        to = lax.rem(g + k, GRPS)
        return (
            pltpu.make_async_remote_copy(
                src_ref=pex.at[pl.ds(to * 8, 8)], dst_ref=r1.at[g], send_sem=e1s.at[k], recv_sem=e1r.at[g],
                device_id={"grp": to}, device_id_type=MESH,
            ),
            pltpu.make_async_remote_copy(
                src_ref=qb, dst_ref=q1.at[g], send_sem=f1s.at[k], recv_sem=f1r.at[g],
                device_id={"grp": to}, device_id_type=MESH,
            ),
        )

    def grp_arrivals(k):
        d = lax.rem(g + k, GRPS)
        return (
            pltpu.make_async_remote_copy(
                src_ref=pex.at[pl.ds(0, 8)], dst_ref=r1.at[d], send_sem=e1s.at[0], recv_sem=e1r.at[d],
                device_id={"grp": d}, device_id_type=MESH,
            ),
            pltpu.make_async_remote_copy(
                src_ref=qb, dst_ref=q1.at[d], send_sem=f1s.at[0], recv_sem=f1r.at[d],
                device_id={"grp": d}, device_id_type=MESH,
            ),
        )

    for k in range(1, GRPS):
        for cp in grp_copies(k):
            cp.start()
    r1[g] = pex[pl.ds(g * 8, 8)]
    q1[g] = qb[...]
    for k in range(1, GRPS):
        for cp in grp_arrivals(k):
            cp.wait_recv()
    r2s[...] = functools.reduce(lambda a, d: a + r1[d], range(1, GRPS), r1[0])
    q2s[...] = functools.reduce(lambda a, d: a + q1[d], range(1, GRPS), q1[0])

    def row_copies(k):
        to = lax.rem(me + k, ROWS)
        return (
            pltpu.make_async_remote_copy(
                src_ref=r2s.at[to // 2], dst_ref=r2.at[me], send_sem=e2s.at[k], recv_sem=e2r.at[me],
                device_id={"row": to}, device_id_type=MESH,
            ),
            pltpu.make_async_remote_copy(
                src_ref=q2s, dst_ref=q2.at[me], send_sem=f2s.at[k], recv_sem=f2r.at[me],
                device_id={"row": to}, device_id_type=MESH,
            ),
        )

    def row_arrivals(k):
        d = lax.rem(me + k, ROWS)
        return (
            pltpu.make_async_remote_copy(
                src_ref=r2s.at[0], dst_ref=r2.at[d], send_sem=e2s.at[0], recv_sem=e2r.at[d],
                device_id={"row": d}, device_id_type=MESH,
            ),
            pltpu.make_async_remote_copy(
                src_ref=q2s, dst_ref=q2.at[d], send_sem=f2s.at[0], recv_sem=f2r.at[d],
                device_id={"row": d}, device_id_type=MESH,
            ),
        )

    for k in range(1, ROWS):
        for cp in row_copies(k):
            cp.start()
    r2[me] = r2s[me // 2]
    q2[me] = q2s[...]
    for k in range(1, ROWS):
        for cp in row_arrivals(k):
            cp.wait_recv()
    tile = functools.reduce(lambda a, d: a + r2[d], range(1, ROWS), r2[0])
    row_ref[...] = jnp.where(core == 0, tile, pltpu.roll(tile, 64, axis=1))[:, :64]
    for m in range(8):
        a, b = q2[2 * m], q2[2 * m + 1]
        col_ref[:, pl.ds(m * 128, 128)] = jnp.where(lane < 64, a, pltpu.roll(b, 64, axis=1))
        tiles[m] = jnp.where(lane < 64, pltpu.roll(a, 64, axis=1), b)
    mir[pl.ds(0, 8)] = exact(tiles[pl.ds(0, 8)].reshape(64, 128), flip).reshape(8, 8, 128)
    for t in range(8, 16):
        col_ref[:, pl.ds(t * 128, 128)] = jnp.where(lane == 0, mir[(16 - t) % 8], mir[15 - t])

    for c in range(CH):

        def drain(s, _, c=c):
            @pl.when(s < 7)
            def _():
                block(s, 0, c).wait_send()
                block(s, 1, c).wait_send()

            @pl.when(s == 7)
            def _():
                block(7, 1 - core, c).wait_send()

            return 0

        lax.fori_loop(0, 8, drain, 0)
    for k in range(1, ROWS):
        b_copy(k).wait_send()
        m_copy(k).wait_send()
        for cp in row_copies(k):
            cp.wait_send()
    for k in range(1, GRPS):
        for cp in grp_copies(k):
            cp.wait_send()


def local(probes, solves, row_spectra, col_spectra):
    w, d, tw, tb = (jnp.asarray(t) for t in tables())
    dma = pltpu.SemaphoreType.DMA
    vm = pltpu.VMEM
    scratch = [
        vm((2, LOCAL, L2), BF16), vm((2, 2, L2, 256), BF16), vm((LOCAL, sum(WIDTHS)), BF16),
        vm((LOCAL, 128), F32), vm((64, 128), F32), vm((8, L1), F32), vm((8, L2), F32),
        vm((8, 2, 2 * LOCAL, 128), F32), vm((ROWS, 2 * LOCAL, 128), F32),
        vm((LOCAL, 4096), F32), vm((512, 4096), BF16), vm((L1, 128), F32),
        vm((8, 128), F32), vm((ROWS, 8, 128), F32), vm((8, 128), F32), vm((ROWS, 8, 128), F32), vm((16, 1024), F32), vm((8, 2048), F32),
        vm((32, L1), BF16), vm((64, 8, 128), F32), vm((64, 8, 128), F32), vm((64, 8, 128), F32), vm((8, 128), F32),
        vm((GRPS, 8, 8, 128), F32), vm((GRPS, 8, 128), F32), vm((8, 8, 128), F32), vm((ROWS, 8, 128), F32),
        vm((8, 128), F32), vm((ROWS, 8, 128), F32),
        dma((7,)), dma((2,)), dma((CH, ROWS)), dma((CH, ROWS)), dma, dma((ROWS,)), dma((ROWS,)), dma((ROWS,)), dma((ROWS,)),
        dma((GRPS,)), dma((GRPS,)), dma((GRPS,)), dma((GRPS,)),
        dma((ROWS,)), dma((ROWS,)), dma((ROWS,)), dma((ROWS,)),
    ]
    hbm = pl.BlockSpec(memory_space=pl.ANY)
    return pl.pallas_call(
        kernel,
        out_shape=(jax.ShapeDtypeStruct((HYPER, 64), F32), jax.ShapeDtypeStruct((HYPER, L2), F32)),
        in_specs=[hbm] * 8,
        out_specs=(pl.BlockSpec(memory_space=pltpu.VMEM), pl.BlockSpec(memory_space=pltpu.VMEM)),
        scratch_shapes=scratch,
        compiler_params=pltpu.CompilerParams(collective_id=0, has_side_effects=True, vmem_limit_bytes=62 << 20),
        name="trace_terms",
    )(probes, solves, row_spectra, col_spectra, w, d, tw, tb)


def solution(mesh):
    placed = (P("grp", "row", None), P("grp", "row", None), P(), P())
    return jax.shard_map(
        local, mesh=mesh, in_specs=placed, out_specs=(P(None, ("grp", "row")), P()), check_vma=False
    )
```

```python
import functools
import math

import jax
import jax.numpy as jnp
import ml_dtypes
import numpy as np
from jax import lax
from jax.experimental import pallas as pl
from jax.experimental.pallas import tpu as pltpu
from jax.sharding import PartitionSpec as P

L1, L2, HYPER, PROBES = 8192, 2048, 8, 8
ROWS, GRPS = 16, 8
LOCAL = L1 // ROWS
SIZES = (128, 128, 128, 64, 32, 32)
STARTS = tuple(sum(SIZES[:c]) for c in range(len(SIZES)))
CH = len(SIZES)
WIDTHS = tuple((6 if n == 128 else 8) * n for n in SIZES) + (512,)
OFFS = tuple(sum(WIDTHS[:c]) for c in range(len(WIDTHS)))
F32, BF16 = jnp.float32, jnp.bfloat16
MESH = pl.DeviceIdType.MESH
SCALE = 1.0 / (PROBES * L1 * L2)
NT = (((1,), (1,)), ((), ()))
NN = (((1,), (0,)), ((), ()))


def halves(table):
    hi = table.astype(ml_dtypes.bfloat16)
    lo = (table - hi.astype(np.float64)).astype(ml_dtypes.bfloat16)
    return hi, lo


@functools.lru_cache(maxsize=None)
def tables():
    x = np.arange(L2)
    w = np.zeros((8, 2, L2, 256), ml_dtypes.bfloat16)
    for pair in range(8):
        for t in range(2):
            j = (2 * pair + t) * 64 + np.arange(64)
            ang = 2 * math.pi * (x[:, None] * j[None, :] % L2) / L2
            hi, lo = halves(np.concatenate([np.cos(ang), -np.sin(ang)], 1))
            w[pair, 0, :, t * 128 : t * 128 + 128] = hi
            w[pair, 1, :, t * 128 : t * 128 + 128] = lo
    fh = np.arange(LOCAL)
    d = np.zeros((LOCAL, sum(WIDTHS)), ml_dtypes.bfloat16)
    for c, (first, n) in enumerate(zip(STARTS + (384,), SIZES + (128,))):
        r = first + np.arange(n)
        ang = 2 * math.pi * (fh[:, None] * r[None, :] % LOCAL) / LOCAL
        hi, lo = halves(np.concatenate([np.cos(ang), np.sin(ang)], 1))
        parts = [hi, lo] if c == CH else [hi, hi, lo] if n == 128 else [hi, hi, lo, lo]
        d[:, OFFS[c] : OFFS[c] + WIDTHS[c]] = np.concatenate(parts, 1)
    r = np.arange(LOCAL)
    tw = np.zeros((LOCAL, 128), np.float32)
    for f in range(16):
        ang = 2 * math.pi * (r * f % L1) / L1
        tw[:, 2 * f], tw[:, 2 * f + 1] = np.cos(ang), np.sin(ang)
    tb = np.zeros((16, 64, 128), np.float32)
    for f in range(16):
        for dd in range(16):
            tb[f, 2 * dd] = math.cos(2 * math.pi * (dd * f % 16) / 16)
            tb[f, 2 * dd + 1] = math.sin(2 * math.pi * (dd * f % 16) / 16)
        for q in range(4):
            ang = 2 * math.pi * ((q * 128 + np.arange(128)) * f % L1) / L1
            for zu in range(2):
                tb[f, 32 + zu * 4 + q] = np.cos(ang)
                tb[f, 40 + zu * 4 + q] = np.sin(ang)
    return w, d, tw, tb


def split(v):
    hi = v.astype(BF16)
    return hi, (v - hi.astype(F32)).astype(BF16)


def mm(a, b, dims=NN):
    return lax.dot_general(a, b, dims, preferred_element_type=F32)


def exact(a, b):
    return lax.dot_general(a, b, NN, precision=lax.Precision.HIGHEST, preferred_element_type=F32)


def minus_i(v, sign):
    return pltpu.roll(v, 64, axis=1) * sign


def turn(v, m, sign):
    m = m % 16
    if m == 0:
        return v
    if m == 4:
        return minus_i(v, sign)
    return v * math.cos(2 * math.pi * m / 16) + minus_i(v, sign) * math.sin(2 * math.pi * m / 16)


def four(a, b, c, d, sign):
    s, t, u = a + c, a - c, b + d
    v = minus_i(b - d, sign)
    return s + u, t + v, s - u, t - v


def kernel(
    z_hbm, u_hbm, rs_hbm, cs_hbm, w_hbm, d_hbm, tw_hbm, tb_hbm,
    row_ref, col_ref,
    x, wbuf, dt, tw, tb, rs, cs, send, recv, acc, yy, cross,
    bs, brecv, ms, mrecv, lb, upm, r32, tiles, mir, pex, qb, r1, q1, r2s, r2, q2s, q2,
    xsem, lsem, wsem, ssem, rsem, own, bss, brs, mss, mrs, e1s, e1r, f1s, f1r, e2s, e2r, f2s, f2r,
):
    me, g = lax.axis_index("row"), lax.axis_index("grp")
    xh, y, core = me // 8, (me // 2) % 4, me % 2
    barrier = pltpu.get_barrier_semaphore()
    for k in range(1, ROWS):
        pl.semaphore_signal(barrier, inc=1, device_id={"row": lax.rem(me + k, ROWS)}, device_id_type=MESH)
    for k in range(1, GRPS):
        pl.semaphore_signal(barrier, inc=1, device_id={"grp": lax.rem(g + k, GRPS)}, device_id_type=MESH)

    def pair_of(s):
        m = s % 4
        dy = (2 + 3 * m + 3 * (m * (m - 1) // 2)) % 4
        return lax.rem(xh + 1 - s // 4, 2) * 4 + lax.rem(y + dy, 4)

    def w_copy(s, slot):
        return pltpu.make_async_copy(w_hbm.at[pair_of(s)], wbuf.at[slot], wsem.at[slot])

    fields = []
    for c in range(CH):
        for zu, field in enumerate((z_hbm, u_hbm)):
            at = pl.ds(2 * STARTS[c] + zu * SIZES[c], SIZES[c])
            fields.append(
                pltpu.make_async_copy(field.at[0, pl.ds(STARTS[c], SIZES[c])], x.at[at], xsem.at[2 * c + zu])
            )
    loads = [
        pltpu.make_async_copy(d_hbm, dt, lsem.at[0]),
        pltpu.make_async_copy(tw_hbm, tw, lsem.at[1]),
        pltpu.make_async_copy(tb_hbm.at[me], tb, lsem.at[2]),
        pltpu.make_async_copy(rs_hbm, rs, lsem.at[3]),
        pltpu.make_async_copy(cs_hbm, cs, lsem.at[4]),
    ]
    for cp in fields[:4]:
        cp.start()
    w_copy(0, 0).start()
    for cp in fields[4:]:
        cp.start()

    def span(c):
        return pl.ds(2 * STARTS[c], 2 * SIZES[c])

    def block(s, t, c):
        return pltpu.make_async_remote_copy(
            src_ref=send.at[s, t, span(c)], dst_ref=recv.at[me, span(c)], send_sem=ssem.at[c, 2 * s + t],
            recv_sem=rsem.at[c, me], device_id={"row": 2 * pair_of(s) + t}, device_id_type=MESH,
        )

    def arrival(c, d):
        return pltpu.make_async_remote_copy(
            src_ref=send.at[0, 0, span(c)], dst_ref=recv.at[d, span(c)], send_sem=ssem.at[c, 0],
            recv_sem=rsem.at[c, d], device_id={"row": d}, device_id_type=MESH,
        )

    def start_block(s, c):
        @pl.when(s < 7)
        def _():
            block(s, 0, c).start()
            block(s, 1, c).start()

        @pl.when(s == 7)
        def _():
            block(7, 1 - core, c).start()

    lane = lax.broadcasted_iota(jnp.int32, (8, 128), 1)
    sub = lax.broadcasted_iota(jnp.int32, (128, 128), 0)
    lan = lax.broadcasted_iota(jnp.int32, (128, 128), 1)

    def b_copy(k):
        return pltpu.make_async_remote_copy(
            src_ref=bs, dst_ref=brecv.at[me], send_sem=bss.at[k], recv_sem=brs.at[me],
            device_id={"row": lax.rem(me + k, ROWS)}, device_id_type=MESH,
        )

    def middle_sums():
        parity = lax.broadcasted_iota(jnp.int32, (L2, 128), 0) % 2
        alt = (1 - 2 * parity).astype(F32).astype(BF16)
        summed = mm(x[...], alt)
        for zu in range(2):
            for q in range(4):
                total = jnp.zeros((1, 128), F32)
                for first, n in zip(STARTS, SIZES):
                    if first // 128 == q:
                        here = summed[2 * first + zu * n : 2 * first + zu * n + n]
                        total = total + jnp.sum(
                            jnp.where(sub[:n] + first % 128 == lan[:n], here, 0.0), axis=0, keepdims=True
                        )
                bs[pl.ds(zu * 4 + q, 1)] = total
        for k in range(1, ROWS):
            b_copy(k).start()

    def drain(c, s, _):
        @pl.when(s < 7)
        def _():
            block(s, 0, c).wait_send()
            block(s, 1, c).wait_send()

        @pl.when(s == 7)
        def _():
            block(7, 1 - core, c).wait_send()

        return 0

    for cp in fields:
        cp.wait()
    pl.semaphore_wait(barrier, ROWS - 1 + GRPS - 1)

    def part(s, slot, first):
        rows = x[pl.ds(first, LOCAL)]
        got = mm(rows, wbuf[slot, 0]) + mm(rows, wbuf[slot, 1])
        for t in range(2):
            send[s, t, pl.ds(first, LOCAL)] = got[:, t * 128 : (t + 1) * 128]

    def section(s, _):
        slot = lax.rem(s, 2)
        w_copy(s, slot).wait()
        w_copy(s + 1, 1 - slot).start()
        part(s, slot, 0)
        part(s, slot, LOCAL)
        block(s, 0, 0).start()
        block(s, 1, 0).start()
        return 0

    w_copy(0, 0).wait()
    w_copy(1, 1).start()
    part(0, 0, 0)
    part(0, 0, LOCAL)
    block(0, 0, 0).start()
    block(0, 1, 0).start()
    section(1, 0)
    middle_sums()
    lax.fori_loop(2, 7, section, 0)
    w_copy(7, 1).wait()
    part(7, 1, 0)
    part(7, 1, LOCAL)
    block(7, 1 - core, 0).start()
    for c in range(1, 3):
        lax.fori_loop(0, 8, lambda s, _, c=c: (start_block(s, c), 0)[1], 0)
    for cp in loads:
        cp.start()
    mine = pltpu.make_async_copy(send.at[7, core], recv.at[me], own)
    mine.start()


    for cp in loads:
        cp.wait()
    flip = (lax.rem(sub + lan, 128) == 0).astype(F32).astype(BF16)

    def flipped(v):
        hi, lo = split(v)
        return mm(hi, flip) + mm(lo, flip)


    def stack_r(t, _):
        tiles[t] = rs[:, pl.ds(pl.multiple_of(t * 128, 128), 128)]
        return 0

    lax.fori_loop(0, 64, stack_r, 0)
    mir[...] = flipped(tiles[...].reshape(512, 128)).reshape(64, 8, 128)

    def put_r(t, _):
        back = jnp.where(lane == 0, mir[lax.rem(64 - t, 64)], mir[63 - t])
        both = jnp.concatenate([tiles[t], back], axis=0)
        hi, lo = split(both)
        at = pl.ds(pl.multiple_of(t * 128, 128), 128)
        r32[pl.ds(0, 16), at] = hi
        r32[pl.ds(16, 16), at] = lo
        return 0

    lax.fori_loop(0, 64, put_r, 0)

    def own_half(tile):
        other = pltpu.roll(tile, 64, axis=1)
        low = lane < 64
        return jnp.where(core == 0, jnp.where(low, tile, other), jnp.where(low, other, tile))

    at = me // 2
    c_here = cs[:, pl.ds(pl.multiple_of(at * 128, 128), 128)]
    c_a = cs[:, pl.ds(pl.multiple_of((15 - at) * 128, 128), 128)]
    c_b = cs[:, pl.ds(pl.multiple_of(lax.rem(16 - at, 16) * 128, 128), 128)]
    c_back = jnp.where(lane == 0, flipped(c_b), flipped(c_a))
    c_back = own_half(c_back)
    c_back = jnp.where(jnp.logical_and(me == 0, lax.rem(lane, 64) == 0), 0.0, c_back)
    c_hi, c_lo = split(jnp.concatenate([own_half(c_here), c_back], axis=0))
    c_both = jnp.concatenate([c_hi, c_lo], axis=0)

    for k in range(1, ROWS):
        d = lax.rem(me + k, ROWS)
        pltpu.make_async_remote_copy(
            src_ref=bs, dst_ref=brecv.at[d], send_sem=bss.at[0], recv_sem=brs.at[d],
            device_id={"row": d}, device_id_type=MESH,
        ).wait_recv()
    brecv[me] = bs[...]
    re = jnp.zeros((8, 128), F32)
    im = jnp.zeros((8, 128), F32)
    for d in range(ROWS):
        re = re + brecv[d] * tb[pl.ds(2 * d, 1)]
        im = im - brecv[d] * tb[pl.ds(2 * d + 1, 1)]
    tc, ts = tb[pl.ds(32, 8)], tb[pl.ds(40, 8)]
    bs2_re = re * tc + im * ts
    bs2_im = im * tc - re * ts
    lb[...] = jnp.zeros_like(lb)
    for q in range(4):
        for zu in range(2):
            a = bs2_re[zu * 4 + q : zu * 4 + q + 1]
            b = bs2_im[zu * 4 + q : zu * 4 + q + 1]
            lb[pl.ds(zu, 1), pl.ds(q * 256, 128)] = a
            lb[pl.ds(zu, 1), pl.ds(q * 256 + 128, 128)] = b
            lb[pl.ds(2 + zu, 1), pl.ds(q * 256, 128)] = b
            lb[pl.ds(2 + zu, 1), pl.ds(q * 256 + 128, 128)] = -a
    mid = jnp.zeros((16, LOCAL), F32)
    for q in range(4):
        hi, lo = split(lb[:, q * 256 : (q + 1) * 256])
        at = OFFS[q] if q < 3 else OFFS[CH]
        d_hi = dt[:, at : at + 256]
        d_lo = dt[:, at + WIDTHS[q if q < 3 else CH] - 256 : at + WIDTHS[q if q < 3 else CH]]
        mid = mid + mm(hi, d_hi, NT) + mm(lo, d_hi, NT) + mm(hi, d_lo, NT)
    mid_cross = mid[0:1] * mid[1:2] + mid[2:3] * mid[3:4]
    lb[...] = jnp.zeros_like(lb)
    for q in range(4):
        lb[pl.ds(q, 1), pl.ds(0, 128)] = mid_cross[:, q * 128 : (q + 1) * 128]
    spread = (
        lax.broadcasted_iota(jnp.int32, (128, 2048), 1) == 16 * lax.broadcasted_iota(jnp.int32, (128, 2048), 0) + me
    ).astype(F32)
    upm[...] = exact(lb[pl.ds(0, 8), pl.ds(0, 128)], spread)
    c_mid = jnp.broadcast_to(cs[:, 1024:1025], (8, 128))
    total = jnp.zeros((8, 128), F32)
    for q in range(4):

        def put_mid(t, total, q=q):
            up = upm[pl.ds(q, 1), pl.ds(pl.multiple_of(t * 128, 128), 128)]
            pex[q * 16 + t] = c_mid * up
            return total + tiles[q * 16 + t] * up

        total = lax.fori_loop(0, 16, put_mid, total)
    ms[...] = jnp.broadcast_to(jnp.sum(total, axis=1, keepdims=True), (8, 128))

    def m_copy(k):
        return pltpu.make_async_remote_copy(
            src_ref=ms, dst_ref=mrecv.at[me], send_sem=mss.at[k], recv_sem=mrs.at[me],
            device_id={"row": lax.rem(me + k, ROWS)}, device_id_type=MESH,
        )

    for k in range(1, ROWS):
        m_copy(k).start()
    mrecv[me] = ms[...]
    for c in range(3, CH):
        lax.fori_loop(0, 8, lambda s, _, c=c: (start_block(s, c), 0)[1], 0)

    sign = jnp.where(lax.broadcasted_iota(jnp.int32, (16, 128), 1) < 64, 1.0, -1.0).astype(F32)
    mine.wait()

    def turned(c):
        for k in range(1, ROWS):
            arrival(c, lax.rem(me + k, ROWS)).wait_recv()

        n = SIZES[c]

        def rows16(i, _):
            ats = [pl.ds(pl.multiple_of(2 * n * p + i * 16, 16), 16) for p in range(2 if n == 128 else 4)]
            jats = [pl.ds(pl.multiple_of(2 * n * p + n + i * 16, 16), 16) for p in range(2 if n == 128 else 4)]
            coef = tw[pl.ds(pl.multiple_of(STARTS[c] + i * 16, 16), 16)]
            for zu in range(2):
                at = pl.ds(pl.multiple_of(2 * STARTS[c] + zu * n + i * 16, 16), 16)
                v = [recv[d, at] for d in range(ROWS)]
                inner = [four(v[d0], v[d0 + 4], v[d0 + 8], v[d0 + 12], sign) for d0 in range(4)]
                for f0 in range(4):
                    outs = four(*[turn(inner[d0][f0], d0 * f0, sign) for d0 in range(4)], sign)
                    for f1 in range(4):
                        f = f0 + 4 * f1
                        val = outs[f1]
                        jval = minus_i(val, sign)
                        if f:
                            cc = jnp.broadcast_to(coef[:, 2 * f : 2 * f + 1], (16, 128))
                            ss = jnp.broadcast_to(coef[:, 2 * f + 1 : 2 * f + 2], (16, 128))
                            val, jval = val * cc + jval * ss, jval * cc - val * ss
                        cols = pl.ds(f * 256 + zu * 128, 128)
                        for p, (part, jpart) in enumerate(zip(split(val), split(jval))):
                            for copy in range(p, len(ats), 2):
                                yy[ats[copy], cols] = part
                                yy[jats[copy], cols] = jpart
            return 0

        lax.fori_loop(0, n // 16, rows16, 0)

    def product(c, cols):
        at, n = OFFS[c], SIZES[c]
        if n == 128:
            return mm(dt[:, at : at + 512], yy[pl.ds(0, 512), cols]) + mm(dt[:, at + 512 : at + 768], yy[pl.ds(0, 256), cols])
        return mm(dt[:, at : at + 8 * n], yy[pl.ds(0, 8 * n), cols])

    for c in range(CH - 1):
        turned(c)

        def add(n, _, c=c):
            cols = pl.ds(pl.multiple_of(n * 512, 512), 512)
            got = product(c, cols)
            acc[:, cols] = got if c == 0 else acc[:, cols] + got
            return 0

        lax.fori_loop(0, 8, add, 0)
    for k in range(1, ROWS):
        d = lax.rem(me + k, ROWS)
        pltpu.make_async_remote_copy(
            src_ref=ms, dst_ref=mrecv.at[d], send_sem=mss.at[0], recv_sem=mrs.at[d],
            device_id={"row": d}, device_id_type=MESH,
        ).wait_recv()
    middle = functools.reduce(lambda a, d: a + mrecv[d], range(1, ROWS), mrecv[0])

    turned(CH - 1)

    def finish(n, _):
        cols = pl.ds(pl.multiple_of(n * 512, 512), 512)
        got = acc[:, cols] + product(CH - 1, cols)
        for h in range(2):
            cross[pl.ds(2 * n + h, LOCAL, stride=16)] = (
                got[:, h * 256 : h * 256 + 128] * got[:, h * 256 + 128 : h * 256 + 256]
            )
        return 0

    lax.fori_loop(0, 8, finish, 0, unroll=4)

    def contract(n, q):
        at = pl.ds(pl.multiple_of(n * 512, 512), 512)
        hi, lo = split(cross[at])
        a = mm(c_both, hi, NT)
        p = a[:16] + a[16:] + mm(c_hi, lo, NT)
        for i in range(4):
            pex[n * 4 + i] = pex[n * 4 + i] + p[:8, i * 128 : (i + 1) * 128]
            tiles[n * 4 + i] = p[8:, i * 128 : (i + 1) * 128]
        weights = r32[:, at]
        b = mm(weights, hi)
        return q + b[:16] + b[16:] + mm(weights[:16], lo)

    q = lax.fori_loop(0, 16, contract, jnp.zeros((16, 128), F32), unroll=8)
    q = q + pltpu.roll(q, 64, axis=1)
    q = jnp.where(lane < 64, q[:8], q[8:])
    qb[...] = jnp.where(jnp.logical_and(me == 0, lane == 64), middle, q) * SCALE
    mir[...] = flipped(tiles[...].reshape(512, 128)).reshape(64, 8, 128)

    def join(t, _):
        back = jnp.where(lane == 0, mir[lax.rem(64 - t, 64)], mir[63 - t])
        pex[t] = (pex[t] + back) * SCALE
        return 0

    lax.fori_loop(0, 64, join, 0, unroll=16)

    def grp_copies(k):
        to = lax.rem(g + k, GRPS)
        return (
            pltpu.make_async_remote_copy(
                src_ref=pex.at[pl.ds(to * 8, 8)], dst_ref=r1.at[g], send_sem=e1s.at[k], recv_sem=e1r.at[g],
                device_id={"grp": to}, device_id_type=MESH,
            ),
            pltpu.make_async_remote_copy(
                src_ref=qb, dst_ref=q1.at[g], send_sem=f1s.at[k], recv_sem=f1r.at[g],
                device_id={"grp": to}, device_id_type=MESH,
            ),
        )

    def grp_arrivals(k):
        d = lax.rem(g + k, GRPS)
        return (
            pltpu.make_async_remote_copy(
                src_ref=pex.at[pl.ds(0, 8)], dst_ref=r1.at[d], send_sem=e1s.at[0], recv_sem=e1r.at[d],
                device_id={"grp": d}, device_id_type=MESH,
            ),
            pltpu.make_async_remote_copy(
                src_ref=qb, dst_ref=q1.at[d], send_sem=f1s.at[0], recv_sem=f1r.at[d],
                device_id={"grp": d}, device_id_type=MESH,
            ),
        )

    for k in range(1, GRPS):
        for cp in grp_copies(k):
            cp.start()
    for c in range(CH):
        lax.fori_loop(0, 8, functools.partial(drain, c), 0)
    r1[g] = pex[pl.ds(g * 8, 8)]
    q1[g] = qb[...]
    for k in range(1, GRPS):
        for cp in grp_arrivals(k):
            cp.wait_recv()
    r2s[...] = functools.reduce(lambda a, d: a + r1[d], range(1, GRPS), r1[0])
    q2s[...] = functools.reduce(lambda a, d: a + q1[d], range(1, GRPS), q1[0])

    def row_copies(k):
        to = lax.rem(me + k, ROWS)
        return (
            pltpu.make_async_remote_copy(
                src_ref=r2s.at[to // 2], dst_ref=r2.at[me], send_sem=e2s.at[k], recv_sem=e2r.at[me],
                device_id={"row": to}, device_id_type=MESH,
            ),
            pltpu.make_async_remote_copy(
                src_ref=q2s, dst_ref=q2.at[me], send_sem=f2s.at[k], recv_sem=f2r.at[me],
                device_id={"row": to}, device_id_type=MESH,
            ),
        )

    def row_arrivals(k):
        d = lax.rem(me + k, ROWS)
        return (
            pltpu.make_async_remote_copy(
                src_ref=r2s.at[0], dst_ref=r2.at[d], send_sem=e2s.at[0], recv_sem=e2r.at[d],
                device_id={"row": d}, device_id_type=MESH,
            ),
            pltpu.make_async_remote_copy(
                src_ref=q2s, dst_ref=q2.at[d], send_sem=f2s.at[0], recv_sem=f2r.at[d],
                device_id={"row": d}, device_id_type=MESH,
            ),
        )

    for k in range(1, ROWS):
        for cp in row_copies(k):
            cp.start()
    for k in range(1, ROWS):
        b_copy(k).wait_send()
        m_copy(k).wait_send()
    for k in range(1, GRPS):
        for cp in grp_copies(k):
            cp.wait_send()
    r2[me] = r2s[me // 2]
    q2[me] = q2s[...]
    for k in range(1, ROWS):
        for cp in row_arrivals(k):
            cp.wait_recv()
    tile = functools.reduce(lambda a, d: a + r2[d], range(1, ROWS), r2[0])
    row_ref[...] = jnp.where(core == 0, tile, pltpu.roll(tile, 64, axis=1))[:, :64]
    for m in range(8):
        a, b = q2[2 * m], q2[2 * m + 1]
        col_ref[:, pl.ds(m * 128, 128)] = jnp.where(lane < 64, a, pltpu.roll(b, 64, axis=1))
        tiles[m] = jnp.where(lane < 64, pltpu.roll(a, 64, axis=1), b)
    mir[pl.ds(0, 8)] = flipped(tiles[pl.ds(0, 8)].reshape(64, 128)).reshape(8, 8, 128)
    for t in range(8, 16):
        col_ref[:, pl.ds(t * 128, 128)] = jnp.where(lane == 0, mir[(16 - t) % 8], mir[15 - t])

    for k in range(1, ROWS):
        for cp in row_copies(k):
            cp.wait_send()


def local(probes, solves, row_spectra, col_spectra):
    w, d, tw, tb = (jnp.asarray(t) for t in tables())
    dma = pltpu.SemaphoreType.DMA
    vm = pltpu.VMEM
    scratch = [
        vm((2 * LOCAL, L2), BF16), vm((2, 2, L2, 256), BF16), vm((LOCAL, sum(WIDTHS)), BF16),
        vm((LOCAL, 128), F32), vm((64, 128), F32), vm((8, L1), F32), vm((8, L2), F32),
        vm((8, 2, 2 * LOCAL, 128), F32), vm((ROWS, 2 * LOCAL, 128), F32),
        vm((LOCAL, 4096), F32), vm((512, 4096), BF16), vm((L1, 128), F32),
        vm((8, 128), F32), vm((ROWS, 8, 128), F32), vm((8, 128), F32), vm((ROWS, 8, 128), F32), vm((16, 1024), F32), vm((8, 2048), F32),
        vm((32, L1), BF16), vm((64, 8, 128), F32), vm((64, 8, 128), F32), vm((64, 8, 128), F32), vm((8, 128), F32),
        vm((GRPS, 8, 8, 128), F32), vm((GRPS, 8, 128), F32), vm((8, 8, 128), F32), vm((ROWS, 8, 128), F32),
        vm((8, 128), F32), vm((ROWS, 8, 128), F32),
        dma((2 * CH,)), dma((5,)), dma((2,)), dma((CH, ROWS)), dma((CH, ROWS)), dma, dma((ROWS,)), dma((ROWS,)), dma((ROWS,)), dma((ROWS,)),
        dma((GRPS,)), dma((GRPS,)), dma((GRPS,)), dma((GRPS,)),
        dma((ROWS,)), dma((ROWS,)), dma((ROWS,)), dma((ROWS,)),
    ]
    hbm = pl.BlockSpec(memory_space=pl.ANY)
    return pl.pallas_call(
        kernel,
        out_shape=(jax.ShapeDtypeStruct((HYPER, 64), F32), jax.ShapeDtypeStruct((HYPER, L2), F32)),
        in_specs=[hbm] * 8,
        out_specs=(pl.BlockSpec(memory_space=pltpu.VMEM), pl.BlockSpec(memory_space=pltpu.VMEM)),
        scratch_shapes=scratch,
        compiler_params=pltpu.CompilerParams(collective_id=0, has_side_effects=True, vmem_limit_bytes=62 << 20),
        name="trace_terms",
    )(probes, solves, row_spectra, col_spectra, w, d, tw, tb)


def solution(mesh):
    placed = (P("grp", "row", None), P("grp", "row", None), P(), P())
    return jax.shard_map(
        local, mesh=mesh, in_specs=placed, out_specs=(P(None, ("grp", "row")), P()), check_vma=False
    )
```
